32 devices in a mesh: groups: 2 (over y), col: 4 (over z), row: 2 (over x), rhs: 2 (over core).
Axes of the slice: x: 2, y: 2, z: 4, core: 2. Of those that a mesh axis runs over, the one named last changes fastest.
Arguments:
- prev_panel: float32 [4, 2048, 4096], P(None, 'row', 'col'), may hold values from -0.09375 to 0.09375
- lower_panel: float32 [3, 2048, 3, 2048], P(None, 'row', None, 'col'), may hold values from -0.125 to 0.125
- solved_prev: float32 [4096, 1024], P('col', ('groups', 'rhs')), parts along dimension 1, may hold values from -6 to 6
- right_block: float32 [8, 2048, 512], P('groups', 'row', 'rhs'), parts along dimension 0, may hold values from -6 to 6
- block_inverse: float32 [4, 2048, 2048], P(None, 'col', 'row'), may hold values from -1 to 1, as said below
Outputs:
- solved: float32 [8, 2048, 512], P('groups', 'col', 'rhs'), parts along dimension 0
The draws below stay inside these ranges and needn't reach their ends.
There are 2 independent parts, one for each index of `groups`. The reference program is written for one: setup_inputs(seed, part) draws one part's arguments, and reference() takes and returns one part's arrays. A program takes and returns all parts, laid end to end along the dimension named above; an argument that names none is the same for every part. Nothing has to cross between parts.
Inputs may be any that keep to these rules, and one draw needn't show every extreme that they name: Each block_inverse[k] is lower triangular with diagonal entries from 0.5 to 1.
All inputs are finite; a program needn't handle non-finite values.
Results may differ from the reference program's by a relative error of at most 0.0001.
Values sent between devices are 32-bit elements; how exact they have to be, the bound alone decides.
A program may use at most 128 MiB of HBM per device.

```python
import jax
import jax.numpy as jnp
from jax import lax

NB = 2048
NBLK = 4
M = 512
PREV = 4096


def draw_block_inverse(key, part):
    first_key, second_key = jax.random.split(jax.random.fold_in(key, 17))
    spread = jax.random.uniform(first_key, (NBLK, NB, NB), jnp.float32, -1.0, 1.0) * (0.9 / jnp.sqrt(jnp.float32(NB)))
    diagonal = jax.random.uniform(second_key, (NBLK, NB), jnp.float32, 0.5, 1.0)
    places = jnp.arange(NB)
    below = places[:, None] > places[None, :]
    same = places[:, None] == places[None, :]
    return jnp.where(below[None], spread, 0.0) + jnp.where(same[None], diagonal[:, :, None], 0.0)


def block_levels(stream_key, dims, cuts, least, top_value):
    factor_of, own = 1.0, jax.random.fold_in(stream_key, 6)
    for dim, parts in cuts:
        draws = jnp.exp(jax.random.uniform(jax.random.fold_in(own, dim), (parts,), jnp.float32, least / len(cuts), top_value / len(cuts)))
        factor_of = factor_of * jnp.repeat(draws, dims[dim] // parts).reshape([-1 if axis == dim else 1 for axis in range(len(dims))])
    return factor_of


def gaussian(key, shape, scale, most, cuts=(), kind=jnp.bfloat16):
    level = block_levels(key, shape, cuts, -0.22, 0.18) if cuts else 1.0
    drawn = jax.random.normal(key, shape, jnp.float32) * scale * level
    return jnp.minimum(jnp.maximum(drawn, -most), most).astype(kind)


def setup_inputs(seed: int = 0, part: int = 0) -> dict:
    key_list = jax.random.split(jax.random.key(seed), 6)
    own_keys = jax.random.split(jax.random.fold_in(key_list[5], part), 6)
    return {
        "prev_panel": gaussian(key_list[0], (NBLK, NB, PREV), PREV ** -0.5, 0.09375, ((1, 2), (2, 4)), jnp.float32),
        "lower_panel": gaussian(key_list[1], (NBLK - 1, NB, NBLK - 1, NB), NB ** -0.5, 0.125, ((1, 2), (3, 4)), jnp.float32),
        "solved_prev": gaussian(own_keys[2], (PREV, M), 1.0, 6.0, ((0, 4), (1, 2)), jnp.float32),
        "right_block": gaussian(own_keys[3], (NBLK, NB, M), 1.0, 6.0, ((1, 2), (2, 2)), jnp.float32),
        "block_inverse": draw_block_inverse(jax.random.fold_in(key_list[5], 71), part),
    }


def product(left, right):
    return jnp.dot(left, right, precision=lax.Precision.HIGHEST, preferred_element_type=jnp.float32)


def reference(prev_panel, lower_panel, solved_prev, right_block, block_inverse):
    solved = []
    for block in range(NBLK):
        partial_value = product(prev_panel[block], solved_prev)
        for earlier in range(block):
            partial_value = partial_value + product(lower_panel[block - 1, :, earlier, :], solved[earlier])
        residual = right_block[block] - partial_value
        solved.append(product(block_inverse[block], residual))
    return jnp.stack(solved)
```

```python
import functools

import jax
import jax.numpy as jnp
from jax import lax
from jax.experimental import pallas as pl
from jax.experimental.pallas import tpu as pltpu
from jax.sharding import PartitionSpec as P

F32, BF16 = jnp.float32, jnp.bfloat16
MESH = pl.DeviceIdType.MESH
HOP, LAM, XLAT = 3, 5, 6


def split(value):
    high = value.astype(BF16)
    return high, (value - high.astype(F32)).astype(BF16)


def product(left, both):
    high, low = split(left)
    n = both.shape[1] // 2
    wide = jnp.dot(high, both, preferred_element_type=F32)
    return wide[:, :n] + wide[:, n:] + jnp.dot(low, both[:, :n], preferred_element_type=F32)


def shape_plan(C, R, NR, NC):
    CR = min(64, NR)
    S = NR // CR
    G = min(4, S)
    QR, Q = CR * G, S // G
    SB = min(256, NC)
    need = 0
    for c in range(C):
        rho, lam = HOP * c, LAM + HOP * (C - 1 - c)
        omega = rho if c == 0 else lam if c == C - 1 else min(rho, lam)
        sigma = rho if c == C - 1 else max(rho, lam)
        kappa = G * min(Q, -(-(c + 1) * NC // QR)) - 1 + sigma + XLAT
        need = max(need, -(-(kappa - omega) // 2))
    return CR, S, G, SB, max(S, need)


def kernel(
    C, R, CR, S, G, SB, D,
    prev_hbm, lower_hbm, sprev_hbm, right_hbm, inv_hbm, out_ref,
    prev, lower, sprev, inv, sprev_both, part, from_l, from_r, to_l, to_r,
    xsend, xrecv, solved, tot, acc,
    prev_sem, lower_sem, sprev_sem, right_sem, inv_sem,
    send_r, recv_l, send_l, recv_r, xs_sem, xr_sem,
):
    T, NR, MH = part.shape
    B = T // 2
    NC = out_ref.shape[1]
    Q, QR, NS = S // G, CR * G, NC // SB
    c, r = lax.axis_index("col"), lax.axis_index("row")
    has_l, has_r = c > 0, c < C - 1
    left, right_of = jnp.maximum(c - 1, 0), jnp.minimum(c + 1, C - 1)

    def need_of(col, row):
        rows = jnp.maximum((col + 1) * NC - row * NR, 0)
        return jnp.minimum(lax.div(rows + QR - 1, QR), Q)

    need, need_l = need_of(c, r), jnp.where(has_l, need_of(c - 1, r), 0)
    rho, lam = HOP * c, LAM + HOP * (C - 1 - c)
    omega = jnp.where(c == 0, rho, jnp.where(has_r, jnp.minimum(rho, lam), lam))
    sigma = jnp.where(has_r, jnp.maximum(rho, lam), rho)
    kappa = G * need_of(c, 0) - 1 + sigma + XLAT
    ticks = (T - 1) * D + 1 + jnp.maximum(kappa, S - 1 + jnp.maximum(rho, lam))

    def rows(q):
        return pl.ds(pl.multiple_of(q * QR, QR), QR)

    def piece_rows(i):
        return pl.ds(pl.multiple_of(i * CR, CR), CR)

    def tri(k, j):
        return lax.div(k * (k - 1), 2) + j

    def load_prev(k, q):
        slot = lax.rem(k, 2)
        return pltpu.make_async_copy(prev_hbm.at[k, rows(q)], prev.at[slot, rows(q)], prev_sem.at[slot, q])

    def load_right(t):
        cols = pl.ds(pl.multiple_of(lax.rem(t, 2) * MH, MH), MH)
        return pltpu.make_async_copy(right_hbm.at[lax.div(t, 2), :, cols], from_l.at[t], right_sem.at[t])

    def load_inv(k, q):
        return pltpu.make_async_copy(inv_hbm.at[k, :, rows(q)], inv.at[k, q], inv_sem.at[k, q])

    def load_lower(k, j):
        return pltpu.make_async_copy(lower_hbm.at[k - 1, j], lower.at[tri(k, j)], lower_sem.at[tri(k, j)])

    def loop(n, body, start=0):
        lax.fori_loop(start, n, lambda i, _: (body(i), 0)[1], 0)

    load_sprev = pltpu.make_async_copy(sprev_hbm, sprev, sprev_sem)
    load_sprev.start()
    loop(Q, lambda q: load_prev(0, q).start())

    @pl.when(c == 0)
    def _():
        load_right(0).start()
        load_right(1).start()

    barrier = pltpu.get_barrier_semaphore()

    @pl.when(has_l)
    def _():
        pl.semaphore_signal(barrier, inc=1, device_id={"col": left}, device_id_type=MESH)

    @pl.when(has_r)
    def _():
        pl.semaphore_signal(barrier, inc=1, device_id={"col": right_of}, device_id_type=MESH)

    for d in range(1, R):
        pl.semaphore_signal(barrier, inc=1, device_id={"row": lax.rem(r + d, R)}, device_id_type=MESH)

    def push_right(t, i):
        return pltpu.make_async_remote_copy(
            src_ref=to_r.at[t, piece_rows(i)], dst_ref=from_l.at[t, piece_rows(i)],
            send_sem=send_r.at[t, i], recv_sem=recv_l.at[t, i],
            device_id={"col": right_of}, device_id_type=MESH)

    def push_left(t, i):
        return pltpu.make_async_remote_copy(
            src_ref=to_l.at[t, piece_rows(i)], dst_ref=from_r.at[t, piece_rows(i)],
            send_sem=send_l.at[t, i], recv_sem=recv_r.at[t, i],
            device_id={"col": left}, device_id_type=MESH)

    def push_x(t, s, d):
        return pltpu.make_async_remote_copy(
            src_ref=xsend.at[t, s], dst_ref=xrecv.at[t, d - 1, s],
            send_sem=xs_sem.at[t, s, d - 1], recv_sem=xr_sem.at[t, s, d - 1],
            device_id={"row": lax.rem(r + d, R)}, device_id_type=MESH)

    def base(k, q):
        load_prev(k, q).wait()
        high, low = split(prev[lax.rem(k, 2), rows(q), :])
        m = sprev_both.shape[1] // 2
        s_hi, s_lo = sprev_both[:, :m], sprev_both[:, m:]
        a = jnp.dot(high, s_hi, preferred_element_type=F32)
        a = a + jnp.dot(high, s_lo, preferred_element_type=F32)
        a = a + jnp.dot(low, s_hi, preferred_element_type=F32)
        part[2 * k, rows(q)] = -a[:, :MH]
        part[2 * k + 1, rows(q)] = -a[:, MH:]

    def less(k, j, h, q):
        part[2 * k + h, rows(q)] -= product(lower[tri(k, j), rows(q), :], solved[j, h])

    load_sprev.wait()
    m = sprev.shape[1]
    s_hi, s_lo = split(sprev[...])
    sprev_both[:, :m] = s_hi
    sprev_both[:, m:] = s_lo
    pl.semaphore_wait(barrier, has_l.astype(jnp.int32) + has_r.astype(jnp.int32) + (R - 1))

    def consume(t):
        k, h = lax.div(t, 2), lax.rem(t, 2)

        @pl.when(need > 0)
        def _():
            for s in range(NS):
                tot[s * SB:(s + 1) * SB] = xsend[t, s]

        @pl.when(need == 0)
        def _():
            tot[:NC] = jnp.zeros((NC, MH), F32)

        for d in range(1, R):
            @pl.when(need_of(c, lax.rem(r + R - d, R)) > 0)
            def _():
                for s in range(NS):
                    push_x(t, s, d).wait_recv()
                    tot[s * SB:(s + 1) * SB] += xrecv[t, d - 1, s]

            @pl.when(need > 0)
            def _():
                for s in range(NS):
                    push_x(t, s, d).wait_send()

        value = tot[:NC]
        solved[k, h, :, :MH], solved[k, h, :, MH:] = split(value)

        @pl.when(h == 0)
        def _():
            out_ref[k, :, :MH] = value

        @pl.when(h == 1)
        def _():
            out_ref[k, :, MH:] = value

    def own(t, q):
        k, h = lax.div(t, 2), lax.rem(t, 2)

        @pl.when(t == 0)
        def _():
            base(0, q)

        @pl.when(k > 0)
        def _():
            @pl.when(jnp.logical_and(h == 0, q == 0))
            def _():
                load_lower(k, k - 1).wait()

            less(k, k - 1, h, q)

    def pass_right(t, i):
        @pl.when(has_l)
        def _():
            push_right(t, i).wait_recv()

        @pl.when(jnp.logical_and(c == 0, i == 0))
        def _():
            load_right(t).wait()

        at = piece_rows(i)
        to_r[t, at] = from_l[t, at] + part[t, at]
        push_right(t, i).start()

        @pl.when(t >= 2)
        def _():
            push_right(t - 2, i).wait_send()

    def pass_left(t, i):
        at = piece_rows(i)

        @pl.when(has_r)
        def _():
            push_left(t, i).wait_recv()
            to_l[t, at] = from_r[t, at] + part[t, at]

        @pl.when(jnp.logical_not(has_r))
        def _():
            to_l[t, at] = part[t, at]

        push_left(t, i).start()

        @pl.when(t >= 2)
        def _():
            push_left(t - 2, i).wait_send()

    def solve(t, q):
        k, h = lax.div(t, 2), lax.rem(t, 2)

        @pl.when(jnp.logical_not(has_r))
        def _():
            for g in range(G):
                push_right(t, q * G + g).wait_recv()

        @pl.when(jnp.logical_and(has_r, q >= need_l))
        def _():
            for g in range(G):
                push_left(t, q * G + g).wait_recv()

        @pl.when(h == 0)
        def _():
            load_inv(k, q).wait()

        tot[:QR] = from_l[t, rows(q)] + part[t, rows(q)]

        @pl.when(has_r)
        def _():
            tot[:QR] += from_r[t, rows(q)]

        high, low = split(tot[:QR])
        piece = product(inv[k, q], jnp.concatenate([high, low], axis=1))

        @pl.when(q == 0)
        def _():
            acc[...] = piece

        @pl.when(q > 0)
        def _():
            acc[...] += piece

        for s in range(NS):
            last = jnp.maximum(c * NC + (s + 1) * SB - r * NR, 1) - 1

            @pl.when(q == jnp.minimum(lax.div(last, QR), Q - 1))
            def _():
                xsend[t, s] = acc[s * SB:(s + 1) * SB]
                for d in range(1, R):
                    push_x(t, s, d).start()

    def fetch(t, i):
        b, h = lax.div(t, 2), lax.rem(t, 2)

        @pl.when(jnp.logical_and(h == 0, i == 1))
        def _():
            @pl.when(b == 0)
            def _():
                loop(need, lambda q: load_inv(0, q).start())
                load_lower(1, 0).start()
                loop(Q, lambda q: load_prev(1, q).start())

            @pl.when(b + 1 < B)
            def _():
                loop(need, lambda q: load_inv(b + 1, q).start())

                @pl.when(c == 0)
                def _():
                    load_right(t + 2).start()
                    load_right(t + 3).start()

            @pl.when(b + 2 < B)
            def _():
                loop(b + 2, lambda j: load_lower(b + 2, j).start())

        @pl.when(jnp.logical_and(jnp.logical_and(h == 1, i == 1), b + 2 < B))
        def _():
            loop(Q, lambda q: load_prev(b + 2, q).start())

    def ahead(t, i):
        b, q = lax.div(t, 2), lax.div(i, G)
        nk = b + 1

        @pl.when(lax.rem(i, G) == G // 2)
        def _():
            base(nk, q)

        @pl.when(lax.rem(i, G) == G - 1)
        def _():
            def older(j):
                @pl.when(q == 0)
                def _():
                    load_lower(nk, j).wait()

                less(nk, j, 0, q)
                less(nk, j, 1, q)

            loop(b, older)

    def at_tick(n, offset, body):
        p = jnp.maximum(n - offset, 0)
        t, i = lax.div(p, D), lax.rem(p, D)

        @pl.when(jnp.logical_and(n >= offset, jnp.logical_and(t < T, i < S)))
        def _():
            body(t, i)

    def tick(n):
        @pl.when(jnp.logical_and(n >= kappa, lax.rem(jnp.maximum(n - kappa, 0), D) == 0))
        def _():
            t = lax.div(n - kappa, D)

            @pl.when(t < T)
            def _():
                consume(t)

        def first(t, i):
            @pl.when(lax.rem(i, G) == 0)
            def _():
                own(t, lax.div(i, G))

            fetch(t, i)

        at_tick(n, omega, first)

        @pl.when(has_r)
        def _():
            at_tick(n, rho, pass_right)

        def to_left(t, i):
            @pl.when(lax.div(i, G) < need_l)
            def _():
                pass_left(t, i)

        @pl.when(has_l)
        def _():
            at_tick(n, lam, to_left)

        def finish(t, i):
            q = lax.div(i, G)

            @pl.when(jnp.logical_and(lax.rem(i, G) == G - 1, q < need))
            def _():
                solve(t, q)

        at_tick(n, sigma, finish)

        def later(t, i):
            @pl.when(jnp.logical_and(lax.rem(t, 2) == 1, lax.div(t, 2) < B - 1))
            def _():
                ahead(t, i)

        at_tick(n, omega, later)

    loop(ticks, tick)

    def drain(t):
        @pl.when(has_r)
        def _():
            loop(S, lambda i: push_right(t, i).wait_send())

        @pl.when(has_l)
        def _():
            loop(need_l * G, lambda i: push_left(t, i).wait_send())

    loop(T, drain, T - 2)


def local(C, R, prev_panel, lower_panel, solved_prev, right_block, block_inverse):
    B, NR, KP = prev_panel.shape
    M = solved_prev.shape[1]
    NC, MH = block_inverse.shape[1], M // 2
    CR, S, G, SB, D = shape_plan(C, R, NR, NC)
    T, Q, NS, X = 2 * B, S // G, NC // SB, max(R - 1, 1)
    pairs = B * (B - 1) // 2
    dma = pltpu.SemaphoreType.DMA
    wide = pltpu.VMEM((T, NR, MH), F32)
    return pl.pallas_call(
        functools.partial(kernel, C, R, CR, S, G, SB, D),
        out_shape=jax.ShapeDtypeStruct((B, NC, M), F32),
        in_specs=[pl.BlockSpec(memory_space=pl.ANY)] * 5,
        out_specs=pl.BlockSpec(memory_space=pltpu.VMEM),
        scratch_shapes=[
            pltpu.VMEM((2, NR, KP), F32),
            pltpu.VMEM((pairs, NR, NC), F32),
            pltpu.VMEM((KP, M), F32),
            pltpu.VMEM((B, Q, NC, CR * G), F32),
            pltpu.VMEM((KP, 2 * M), BF16),
            wide, wide, wide, wide, wide,
            pltpu.VMEM((T, NS, SB, MH), F32),
            pltpu.VMEM((T, X, NS, SB, MH), F32),
            pltpu.VMEM((B, 2, NC, 2 * MH), BF16),
            pltpu.VMEM((max(NC, CR * G), MH), F32),
            pltpu.VMEM((NC, MH), F32),
            dma((2, Q)), dma((pairs,)), dma, dma((T,)), dma((B, Q)),
            dma((T, S)), dma((T, S)), dma((T, S)), dma((T, S)),
            dma((T, NS, X)), dma((T, NS, X)),
        ],
        compiler_params=pltpu.CompilerParams(
            collective_id=0, has_side_effects=True, vmem_limit_bytes=63 * 2**20),
    )(prev_panel, jnp.transpose(lower_panel, (0, 2, 1, 3)), solved_prev, right_block, block_inverse)


def solution(mesh):
    return jax.shard_map(
        functools.partial(local, mesh.shape["col"], mesh.shape["row"]),
        mesh=mesh,
        in_specs=(
            P(None, "row", "col"),
            P(None, "row", None, "col"),
            P("col", ("groups", "rhs")),
            P("groups", "row", "rhs"),
            P(None, "col", "row"),
        ),
        out_specs=P("groups", "col", "rhs"),
        check_vma=False,
    )
```

```python
import functools

import jax
import jax.numpy as jnp
from jax import lax
from jax.experimental import pallas as pl
from jax.experimental.pallas import tpu as pltpu
from jax.sharding import PartitionSpec as P

F32, BF16 = jnp.float32, jnp.bfloat16
MESH = pl.DeviceIdType.MESH
HOP = 6
LAM = 5
XLAT = 6


def split(value):
    high = value.astype(BF16)
    return high, (value - high.astype(F32)).astype(BF16)


def product(left, both):
    high, low = split(left)
    n = both.shape[1] // 2
    wide = jnp.dot(high, both, preferred_element_type=F32)
    return wide[:, :n] + wide[:, n:] + jnp.dot(low, both[:, :n], preferred_element_type=F32)


def shape_plan(C, R, NR, NC):
    CR = min(64, NR)
    S = NR // CR
    G = min(4, S)
    QR, Q = CR * G, S // G
    SB = min(256, NC)
    need = 0
    for c in range(C):
        rho, lam = HOP * c, LAM + HOP * (C - 1 - c)
        omega = rho if c == 0 else lam if c == C - 1 else min(rho, lam)
        sigma = rho if c == C - 1 else max(rho, lam)
        kappa = G * min(Q, -(-(c + 1) * NC // QR)) - 1 + sigma + XLAT
        need = max(need, -(-(kappa - omega) // 2))
    return CR, S, G, SB, max(S, need)


def kernel(
    C, R, CR, S, G, SB, D,
    prev_hbm, lower_hbm, sprev_hbm, right_hbm, inv_hbm, out_ref,
    prev, lower, sprev, inv, sprev_both, part, from_l, from_r, to_l, to_r,
    xsend, xrecv, solved, tot, acc,
    prev_sem, lower_sem, sprev_sem, right_sem, inv_sem,
    send_r, recv_l, send_l, recv_r, xs_sem, xr_sem,
):
    T, NR, MH = part.shape
    B = T // 2
    NC = out_ref.shape[1]
    Q, QR, NS = S // G, CR * G, NC // SB
    c, r = lax.axis_index("col"), lax.axis_index("row")
    has_l, has_r = c > 0, c < C - 1
    left, right_of = jnp.maximum(c - 1, 0), jnp.minimum(c + 1, C - 1)

    def need_of(col, row):
        rows = jnp.maximum((col + 1) * NC - row * NR, 0)
        return jnp.minimum(lax.div(rows + QR - 1, QR), Q)

    need, need_l = need_of(c, r), jnp.where(has_l, need_of(c - 1, r), 0)
    rho, lam = HOP * c, LAM + HOP * (C - 1 - c)
    omega = jnp.where(c == 0, rho, jnp.where(has_r, jnp.minimum(rho, lam), lam))
    sigma = jnp.where(has_r, jnp.maximum(rho, lam), rho)
    kappa = G * need_of(c, 0) - 1 + sigma + XLAT
    ticks = (T - 1) * D + 1 + jnp.maximum(kappa, S - 1 + jnp.maximum(rho, lam))

    def rows(q):
        return pl.ds(pl.multiple_of(q * QR, QR), QR)

    def piece_rows(i):
        return pl.ds(pl.multiple_of(i * CR, CR), CR)

    def tri(k, j):
        return lax.div(k * (k - 1), 2) + j

    def load_prev(k, q):
        slot = lax.rem(k, 2)
        return pltpu.make_async_copy(prev_hbm.at[k, rows(q)], prev.at[slot, rows(q)], prev_sem.at[slot, q])

    def load_right(t):
        cols = pl.ds(pl.multiple_of(lax.rem(t, 2) * MH, MH), MH)
        return pltpu.make_async_copy(right_hbm.at[lax.div(t, 2), :, cols], from_l.at[t], right_sem.at[t])

    def load_inv(k, q):
        return pltpu.make_async_copy(inv_hbm.at[k, :, rows(q)], inv.at[k, q], inv_sem.at[k, q])

    def load_lower(k, j):
        return pltpu.make_async_copy(lower_hbm.at[k - 1, j], lower.at[tri(k, j)], lower_sem.at[tri(k, j)])

    def loop(n, body, start=0):
        lax.fori_loop(start, n, lambda i, _: (body(i), 0)[1], 0)

    load_sprev = pltpu.make_async_copy(sprev_hbm, sprev, sprev_sem)
    load_sprev.start()
    loop(Q, lambda q: load_prev(0, q).start())

    @pl.when(c == 0)
    def _():
        load_right(0).start()
        load_right(1).start()

    barrier = pltpu.get_barrier_semaphore()

    @pl.when(has_l)
    def _():
        pl.semaphore_signal(barrier, inc=1, device_id={"col": left}, device_id_type=MESH)

    @pl.when(has_r)
    def _():
        pl.semaphore_signal(barrier, inc=1, device_id={"col": right_of}, device_id_type=MESH)

    for d in range(1, R):
        pl.semaphore_signal(barrier, inc=1, device_id={"row": lax.rem(r + d, R)}, device_id_type=MESH)

    def push_right(t, i):
        return pltpu.make_async_remote_copy(
            src_ref=to_r.at[t, piece_rows(i)], dst_ref=from_l.at[t, piece_rows(i)],
            send_sem=send_r.at[t, i], recv_sem=recv_l.at[t, i],
            device_id={"col": right_of}, device_id_type=MESH)

    def push_left(t, i):
        return pltpu.make_async_remote_copy(
            src_ref=to_l.at[t, piece_rows(i)], dst_ref=from_r.at[t, piece_rows(i)],
            send_sem=send_l.at[t, i], recv_sem=recv_r.at[t, i],
            device_id={"col": left}, device_id_type=MESH)

    def push_x(t, s, d):
        return pltpu.make_async_remote_copy(
            src_ref=xsend.at[t, s], dst_ref=xrecv.at[t, d - 1, s],
            send_sem=xs_sem.at[t, s, d - 1], recv_sem=xr_sem.at[t, s, d - 1],
            device_id={"row": lax.rem(r + d, R)}, device_id_type=MESH)

    def base(k, q):
        load_prev(k, q).wait()
        high, low = split(prev[lax.rem(k, 2), rows(q), :])
        m = sprev_both.shape[1] // 2
        s_hi, s_lo = sprev_both[:, :m], sprev_both[:, m:]
        a = jnp.dot(high, s_hi, preferred_element_type=F32)
        a = a + jnp.dot(high, s_lo, preferred_element_type=F32)
        a = a + jnp.dot(low, s_hi, preferred_element_type=F32)
        part[2 * k, rows(q)] = -a[:, :MH]
        part[2 * k + 1, rows(q)] = -a[:, MH:]

    def less(k, j, h, q):
        part[2 * k + h, rows(q)] -= product(lower[tri(k, j), rows(q), :], solved[j, h])

    load_sprev.wait()
    m = sprev.shape[1]
    s_hi, s_lo = split(sprev[...])
    sprev_both[:, :m] = s_hi
    sprev_both[:, m:] = s_lo
    pl.semaphore_wait(barrier, has_l.astype(jnp.int32) + has_r.astype(jnp.int32) + (R - 1))

    def consume(t):
        k, h = lax.div(t, 2), lax.rem(t, 2)

        @pl.when(need > 0)
        def _():
            for s in range(NS):
                tot[s * SB:(s + 1) * SB] = xsend[t, s]

        @pl.when(need == 0)
        def _():
            tot[:NC] = jnp.zeros((NC, MH), F32)

        for d in range(1, R):
            @pl.when(need_of(c, lax.rem(r + R - d, R)) > 0)
            def _():
                for s in range(NS):
                    push_x(t, s, d).wait_recv()
                    tot[s * SB:(s + 1) * SB] += xrecv[t, d - 1, s]

            @pl.when(need > 0)
            def _():
                for s in range(NS):
                    push_x(t, s, d).wait_send()

        value = tot[:NC]
        solved[k, h, :, :MH], solved[k, h, :, MH:] = split(value)

        @pl.when(h == 0)
        def _():
            out_ref[k, :, :MH] = value

        @pl.when(h == 1)
        def _():
            out_ref[k, :, MH:] = value

    def own(t, q):
        k, h = lax.div(t, 2), lax.rem(t, 2)

        @pl.when(t == 0)
        def _():
            base(0, q)

        @pl.when(k > 0)
        def _():
            @pl.when(jnp.logical_and(h == 0, q == 0))
            def _():
                load_lower(k, k - 1).wait()

            less(k, k - 1, h, q)

    def pass_right(t, i):
        @pl.when(has_l)
        def _():
            push_right(t, i).wait_recv()

        @pl.when(jnp.logical_and(c == 0, i == 0))
        def _():
            load_right(t).wait()

        at = piece_rows(i)
        to_r[t, at] = from_l[t, at] + part[t, at]
        push_right(t, i).start()

        @pl.when(t >= 2)
        def _():
            push_right(t - 2, i).wait_send()

    def pass_left(t, i):
        at = piece_rows(i)

        @pl.when(has_r)
        def _():
            push_left(t, i).wait_recv()
            to_l[t, at] = from_r[t, at] + part[t, at]

        @pl.when(jnp.logical_not(has_r))
        def _():
            to_l[t, at] = part[t, at]

        push_left(t, i).start()

        @pl.when(t >= 2)
        def _():
            push_left(t - 2, i).wait_send()

    def solve(t, q):
        k, h = lax.div(t, 2), lax.rem(t, 2)

        @pl.when(jnp.logical_not(has_r))
        def _():
            for g in range(G):
                push_right(t, q * G + g).wait_recv()

        @pl.when(jnp.logical_and(has_r, q >= need_l))
        def _():
            for g in range(G):
                push_left(t, q * G + g).wait_recv()

        @pl.when(h == 0)
        def _():
            load_inv(k, q).wait()

        tot[:QR] = from_l[t, rows(q)] + part[t, rows(q)]

        @pl.when(has_r)
        def _():
            tot[:QR] += from_r[t, rows(q)]

        high, low = split(tot[:QR])
        piece = product(inv[k, q], jnp.concatenate([high, low], axis=1))

        @pl.when(q == 0)
        def _():
            acc[...] = piece

        @pl.when(q > 0)
        def _():
            acc[...] += piece

        for s in range(NS):
            last = jnp.maximum(c * NC + (s + 1) * SB - r * NR, 1) - 1

            @pl.when(q == jnp.minimum(lax.div(last, QR), Q - 1))
            def _():
                xsend[t, s] = acc[s * SB:(s + 1) * SB]
                for d in range(1, R):
                    push_x(t, s, d).start()

    def fetch(t, i):
        b, h = lax.div(t, 2), lax.rem(t, 2)

        @pl.when(jnp.logical_and(h == 0, i == 1))
        def _():
            @pl.when(b == 0)
            def _():
                loop(need, lambda q: load_inv(0, q).start())
                load_lower(1, 0).start()
                loop(Q, lambda q: load_prev(1, q).start())

            @pl.when(b + 1 < B)
            def _():
                loop(need, lambda q: load_inv(b + 1, q).start())

                @pl.when(c == 0)
                def _():
                    load_right(t + 2).start()
                    load_right(t + 3).start()

            @pl.when(b + 2 < B)
            def _():
                loop(b + 2, lambda j: load_lower(b + 2, j).start())

        @pl.when(jnp.logical_and(jnp.logical_and(h == 1, i == 1), b + 2 < B))
        def _():
            loop(Q, lambda q: load_prev(b + 2, q).start())

    def ahead(t, i):
        b, q = lax.div(t, 2), lax.div(i, G)
        nk = b + 1

        @pl.when(lax.rem(i, G) == G // 2)
        def _():
            base(nk, q)

        @pl.when(lax.rem(i, G) == G - 1)
        def _():
            def older(j):
                @pl.when(q == 0)
                def _():
                    load_lower(nk, j).wait()

                less(nk, j, 0, q)
                less(nk, j, 1, q)

            loop(b, older)

    def at_tick(n, offset, body):
        p = jnp.maximum(n - offset, 0)
        t, i = lax.div(p, D), lax.rem(p, D)

        @pl.when(jnp.logical_and(n >= offset, jnp.logical_and(t < T, i < S)))
        def _():
            body(t, i)

    def tick(n):
        @pl.when(jnp.logical_and(n >= kappa, lax.rem(jnp.maximum(n - kappa, 0), D) == 0))
        def _():
            t = lax.div(n - kappa, D)

            @pl.when(t < T)
            def _():
                consume(t)

        def first(t, i):
            @pl.when(lax.rem(i, G) == 0)
            def _():
                own(t, lax.div(i, G))

            fetch(t, i)

        at_tick(n, omega, first)

        @pl.when(has_r)
        def _():
            at_tick(n, rho, pass_right)

        def to_left(t, i):
            @pl.when(lax.div(i, G) < need_l)
            def _():
                pass_left(t, i)

        @pl.when(has_l)
        def _():
            at_tick(n, lam, to_left)

        def finish(t, i):
            q = lax.div(i, G)

            @pl.when(jnp.logical_and(lax.rem(i, G) == G - 1, q < need))
            def _():
                solve(t, q)

        at_tick(n, sigma, finish)

        def later(t, i):
            @pl.when(jnp.logical_and(lax.rem(t, 2) == 1, lax.div(t, 2) < B - 1))
            def _():
                ahead(t, i)

        at_tick(n, omega, later)

    loop(ticks, tick)

    def drain(t):
        @pl.when(has_r)
        def _():
            loop(S, lambda i: push_right(t, i).wait_send())

        @pl.when(has_l)
        def _():
            loop(need_l * G, lambda i: push_left(t, i).wait_send())

    loop(T, drain, T - 2)


def local(C, R, prev_panel, lower_panel, solved_prev, right_block, block_inverse):
    B, NR, KP = prev_panel.shape
    M = solved_prev.shape[1]
    NC, MH = block_inverse.shape[1], M // 2
    CR, S, G, SB, D = shape_plan(C, R, NR, NC)
    T, Q, NS, X = 2 * B, S // G, NC // SB, max(R - 1, 1)
    pairs = B * (B - 1) // 2
    dma = pltpu.SemaphoreType.DMA
    wide = pltpu.VMEM((T, NR, MH), F32)
    return pl.pallas_call(
        functools.partial(kernel, C, R, CR, S, G, SB, D),
        out_shape=jax.ShapeDtypeStruct((B, NC, M), F32),
        in_specs=[pl.BlockSpec(memory_space=pl.ANY)] * 5,
        out_specs=pl.BlockSpec(memory_space=pltpu.VMEM),
        scratch_shapes=[
            pltpu.VMEM((2, NR, KP), F32),
            pltpu.VMEM((pairs, NR, NC), F32),
            pltpu.VMEM((KP, M), F32),
            pltpu.VMEM((B, Q, NC, CR * G), F32),
            pltpu.VMEM((KP, 2 * M), BF16),
            wide, wide, wide, wide, wide,
            pltpu.VMEM((T, NS, SB, MH), F32),
            pltpu.VMEM((T, X, NS, SB, MH), F32),
            pltpu.VMEM((B, 2, NC, 2 * MH), BF16),
            pltpu.VMEM((max(NC, CR * G), MH), F32),
            pltpu.VMEM((NC, MH), F32),
            dma((2, Q)), dma((pairs,)), dma, dma((T,)), dma((B, Q)),
            dma((T, S)), dma((T, S)), dma((T, S)), dma((T, S)),
            dma((T, NS, X)), dma((T, NS, X)),
        ],
        compiler_params=pltpu.CompilerParams(
            collective_id=0, has_side_effects=True, vmem_limit_bytes=63 * 2**20),
    )(prev_panel, jnp.transpose(lower_panel, (0, 2, 1, 3)), solved_prev, right_block, block_inverse)


def solution(mesh):
    return jax.shard_map(
        functools.partial(local, mesh.shape["col"], mesh.shape["row"]),
        mesh=mesh,
        in_specs=(
            P(None, "row", "col"),
            P(None, "row", None, "col"),
            P("col", ("groups", "rhs")),
            P("groups", "row", "rhs"),
            P(None, "col", "row"),
        ),
        out_specs=P("groups", "col", "rhs"),
        check_vma=False,
    )
```

```python
import functools

import jax
import jax.numpy as jnp
from jax import lax
from jax.experimental import pallas as pl
from jax.experimental.pallas import tpu as pltpu
from jax.sharding import PartitionSpec as P

F32, BF16 = jnp.float32, jnp.bfloat16
MESH = pl.DeviceIdType.MESH
HOP = 6
LAM = 5
XLAT = 8
LAG = 15
STAGGER = 0
VLIM = 59


def split(value):
    high = value.astype(BF16)
    return high, (value - high.astype(F32)).astype(BF16)


def product(left, both):
    high, low = split(left)
    n = both.shape[1] // 2
    wide = jnp.dot(high, both, preferred_element_type=F32)
    return wide[:, :n] + wide[:, n:] + jnp.dot(low, both[:, :n], preferred_element_type=F32)


def shape_plan(C, R, NR, NC):
    CR = min(64, NR)
    S = NR // CR
    G = min(4, S)
    QR, Q = CR * G, S // G
    SB = min(256, NC)
    need = 0
    for c in range(C):
        rho, lam = HOP * c, LAM + HOP * (C - 1 - c)
        omega = rho if c == 0 else lam if c == C - 1 else min(rho, lam)
        sigma = rho if c == C - 1 else max(rho, lam)
        kappa = G * min(Q, -(-(c + 1) * NC // QR)) - 1 + sigma + XLAT
        need = max(need, -(-(kappa - omega) // 2))
    return CR, S, G, SB, max(S, need)


def kernel(
    C, R, H, CR, S, G, SB, D,
    prev_hbm, lower_hbm, sprev_hbm, right_hbm, inv_hbm, out_ref,
    prev, lower, sprev, inv, sprev_both, part, from_l, from_r, to_l, to_r,
    xsend, xrecv, solved, tot, acc,
    prev_sem, lower_sem, sprev_sem, right_sem, inv_sem,
    send_r, recv_l, send_l, recv_r, xs_sem, xr_sem, go_sem,
):
    T, NR, MH = part.shape
    B = T // 2
    NC = out_ref.shape[1]
    Q, QR, NS = S // G, CR * G, NC // SB
    c, r, w = lax.axis_index("col"), lax.axis_index("row"), lax.axis_index("rhs")
    has_l, has_r = c > 0, c < C - 1
    left, right_of = jnp.maximum(c - 1, 0), jnp.minimum(c + 1, C - 1)

    def need_of(col, row):
        rows = jnp.maximum((col + 1) * NC - row * NR, 0)
        return jnp.minimum(lax.div(rows + QR - 1, QR), Q)

    need, need_l = need_of(c, r), jnp.where(has_l, need_of(c - 1, r), 0)
    rho, lam = HOP * c, LAM + HOP * (C - 1 - c)
    omega = jnp.where(c == 0, rho, jnp.where(has_r, jnp.minimum(rho, lam), lam))
    sigma = jnp.where(has_r, jnp.maximum(rho, lam), rho)
    kappa = G * need_of(c, 0) - 1 + sigma + XLAT
    ticks = (T - 1) * D + 1 + jnp.maximum(kappa, S - 1 + jnp.maximum(rho, lam))

    def rows(q):
        return pl.ds(pl.multiple_of(q * QR, QR), QR)

    def piece_rows(i):
        return pl.ds(pl.multiple_of(i * CR, CR), CR)

    def tri(k, j):
        return lax.div(k * (k - 1), 2) + j

    def load_prev(k, q):
        slot = lax.rem(k, 2)
        return pltpu.make_async_copy(prev_hbm.at[k, rows(q)], prev.at[slot, rows(q)], prev_sem.at[slot, q])

    def load_right(t):
        cols = pl.ds(pl.multiple_of(lax.rem(t, 2) * MH, MH), MH)
        return pltpu.make_async_copy(right_hbm.at[lax.div(t, 2), :, cols], from_l.at[t], right_sem.at[t])

    def load_inv(k, q):
        return pltpu.make_async_copy(inv_hbm.at[k, :, rows(q)], inv.at[k, q], inv_sem.at[k, q])

    def load_lower(k, j):
        return pltpu.make_async_copy(lower_hbm.at[k - 1, j], lower.at[tri(k, j)], lower_sem.at[tri(k, j)])

    def loop(n, body, start=0):
        lax.fori_loop(start, n, lambda i, _: (body(i), 0)[1], 0)

    load_sprev = pltpu.make_async_copy(sprev_hbm, sprev, sprev_sem)
    load_sprev.start()
    load_prev(0, 0).start()

    @pl.when(c == 0)
    def _():
        load_right(0).start()

    barrier = pltpu.get_barrier_semaphore()

    @pl.when(has_l)
    def _():
        pl.semaphore_signal(barrier, inc=1, device_id={"col": left}, device_id_type=MESH)

    @pl.when(has_r)
    def _():
        pl.semaphore_signal(barrier, inc=1, device_id={"col": right_of}, device_id_type=MESH)

    for d in range(1, R):
        pl.semaphore_signal(barrier, inc=1, device_id={"row": lax.rem(r + d, R)}, device_id_type=MESH)

    follows, leads = jnp.logical_and(c == 0, w * (H - 1) > 0), jnp.logical_and(c == 0, w < H - 1)
    before, after = jnp.maximum(w - 1, 0), jnp.minimum(w + 1, H - 1)

    @pl.when(follows)
    def _():
        pl.semaphore_signal(barrier, inc=1, device_id={"rhs": before}, device_id_type=MESH)

    @pl.when(leads)
    def _():
        pl.semaphore_signal(barrier, inc=1, device_id={"rhs": after}, device_id_type=MESH)

    def push_right(t, i):
        return pltpu.make_async_remote_copy(
            src_ref=to_r.at[t, piece_rows(i)], dst_ref=from_l.at[t, piece_rows(i)],
            send_sem=send_r.at[t, i], recv_sem=recv_l.at[t, i],
            device_id={"col": right_of}, device_id_type=MESH)

    def push_left(t, i):
        return pltpu.make_async_remote_copy(
            src_ref=to_l.at[t, piece_rows(i)], dst_ref=from_r.at[t, piece_rows(i)],
            send_sem=send_l.at[t, i], recv_sem=recv_r.at[t, i],
            device_id={"col": left}, device_id_type=MESH)

    def push_x(t, s, d):
        return pltpu.make_async_remote_copy(
            src_ref=xsend.at[t, s], dst_ref=xrecv.at[t, d - 1, s],
            send_sem=xs_sem.at[t, s, d - 1], recv_sem=xr_sem.at[t, s, d - 1],
            device_id={"row": lax.rem(r + d, R)}, device_id_type=MESH)

    def base(k, q):
        load_prev(k, q).wait()
        high, low = split(prev[lax.rem(k, 2), rows(q), :])
        m = sprev_both.shape[1] // 2
        s_hi, s_lo = sprev_both[:, :m], sprev_both[:, m:]
        a = jnp.dot(high, s_hi, preferred_element_type=F32)
        a = a + jnp.dot(high, s_lo, preferred_element_type=F32)
        a = a + jnp.dot(low, s_hi, preferred_element_type=F32)
        part[2 * k, rows(q)] = -a[:, :MH]
        part[2 * k + 1, rows(q)] = -a[:, MH:]

    def less(k, j, h, q):
        both = jnp.concatenate([solved[j, h], solved[j, 2 + h]], axis=1)
        part[2 * k + h, rows(q)] -= product(lower[tri(k, j), rows(q), :], both)

    def less_both(k, j, q):
        s_hi = jnp.concatenate([solved[j, 0], solved[j, 1]], axis=1)
        s_lo = jnp.concatenate([solved[j, 2], solved[j, 3]], axis=1)
        high, low = split(lower[tri(k, j), rows(q), :])
        a = jnp.dot(high, s_hi, preferred_element_type=F32)
        a = a + jnp.dot(high, s_lo, preferred_element_type=F32)
        a = a + jnp.dot(low, s_hi, preferred_element_type=F32)
        part[2 * k, rows(q)] -= a[:, :MH]
        part[2 * k + 1, rows(q)] -= a[:, MH:]

    load_sprev.wait()
    loop(Q, lambda q: load_prev(0, q).start(), 1)

    @pl.when(c == 0)
    def _():
        load_right(1).start()

    m = sprev.shape[1]
    s_hi, s_lo = split(sprev[...])
    sprev_both[:, :m] = s_hi
    sprev_both[:, m:] = s_lo
    base(0, 0)
    met = has_l.astype(jnp.int32) + has_r.astype(jnp.int32) + follows.astype(jnp.int32) + leads.astype(jnp.int32)
    pl.semaphore_wait(barrier, met + (R - 1))

    def consume(t):
        k, h = lax.div(t, 2), lax.rem(t, 2)

        @pl.when(need > 0)
        def _():
            for s in range(NS):
                tot[s * SB:(s + 1) * SB] = xsend[t, s]

        @pl.when(need == 0)
        def _():
            tot[:NC] = jnp.zeros((NC, MH), F32)

        for d in range(1, R):
            @pl.when(need_of(c, lax.rem(r + R - d, R)) > 0)
            def _():
                for s in range(NS):
                    push_x(t, s, d).wait_recv()
                    tot[s * SB:(s + 1) * SB] += xrecv[t, d - 1, s]

            @pl.when(need > 0)
            def _():
                for s in range(NS):
                    push_x(t, s, d).wait_send()

        value = tot[:NC]
        for side in range(2):
            @pl.when(h == side)
            def _():
                out_ref[k, :, side * MH:(side + 1) * MH] = value

        solved[k, h], solved[k, 2 + h] = split(value)

    def own(t, q):
        k, h = lax.div(t, 2), lax.rem(t, 2)

        @pl.when(jnp.logical_and(t == 0, q > 0))
        def _():
            base(0, q)

        @pl.when(k > 0)
        def _():
            @pl.when(jnp.logical_and(h == 0, q == 0))
            def _():
                load_lower(k, k - 1).wait()

            less(k, k - 1, h, q)

    last_lead = min(LAG, S - 1)

    def pass_right(t, i):
        @pl.when(has_l)
        def _():
            push_right(t, i).wait_recv()

        @pl.when(jnp.logical_and(c == 0, i == 0))
        def _():
            load_right(t).wait()

        begin = jnp.logical_and(t == 0, i == 0)

        @pl.when(jnp.logical_and(follows, begin))
        def _():
            pl.semaphore_wait(go_sem, 1)

        at = piece_rows(i)
        to_r[t, at] = from_l[t, at] + part[t, at]
        push_right(t, i).start()

        @pl.when(jnp.logical_and(leads, jnp.logical_and(t == 1, i == S // 4)))
        def _():
            push_right(0, last_lead).wait_send()
            pl.semaphore_signal(go_sem, inc=1, device_id={"rhs": after}, device_id_type=MESH)

        skip = jnp.logical_and(leads, jnp.logical_and(t == 2, i == last_lead))

        @pl.when(jnp.logical_and(t >= 2, jnp.logical_not(skip)))
        def _():
            push_right(t - 2, i).wait_send()

    def pass_left(t, i):
        at = piece_rows(i)

        @pl.when(has_r)
        def _():
            push_left(t, i).wait_recv()
            to_l[t, at] = from_r[t, at] + part[t, at]

        @pl.when(jnp.logical_not(has_r))
        def _():
            to_l[t, at] = part[t, at]

        push_left(t, i).start()

        @pl.when(t >= 2)
        def _():
            push_left(t - 2, i).wait_send()

    def solve(t, q):
        k, h = lax.div(t, 2), lax.rem(t, 2)

        @pl.when(jnp.logical_not(has_r))
        def _():
            for g in range(G):
                push_right(t, q * G + g).wait_recv()

        @pl.when(jnp.logical_and(has_r, q >= need_l))
        def _():
            for g in range(G):
                push_left(t, q * G + g).wait_recv()

        @pl.when(h == 0)
        def _():
            load_inv(k, q).wait()

        tot[:QR] = from_l[t, rows(q)] + part[t, rows(q)]

        @pl.when(has_r)
        def _():
            tot[:QR] += from_r[t, rows(q)]

        high, low = split(tot[:QR])
        piece = product(inv[k, q], jnp.concatenate([high, low], axis=1))

        @pl.when(q == 0)
        def _():
            acc[...] = piece

        @pl.when(q > 0)
        def _():
            acc[...] += piece

        for s in range(NS):
            last = jnp.maximum(c * NC + (s + 1) * SB - r * NR, 1) - 1

            @pl.when(q == jnp.minimum(lax.div(last, QR), Q - 1))
            def _():
                xsend[t, s] = acc[s * SB:(s + 1) * SB]
                for d in range(1, R):
                    push_x(t, s, d).start()

    def fetch(t, i):
        b, h = lax.div(t, 2), lax.rem(t, 2)

        @pl.when(jnp.logical_and(h == 0, i == 1))
        def _():
            @pl.when(b == 0)
            def _():
                loop(need, lambda q: load_inv(0, q).start())
                load_lower(1, 0).start()
                loop(Q, lambda q: load_prev(1, q).start())

            @pl.when(b + 1 < B)
            def _():
                loop(need, lambda q: load_inv(b + 1, q).start())

                @pl.when(c == 0)
                def _():
                    load_right(t + 2).start()
                    load_right(t + 3).start()

            @pl.when(b + 2 < B)
            def _():
                loop(b + 2, lambda j: load_lower(b + 2, j).start())

        @pl.when(jnp.logical_and(jnp.logical_and(h == 1, i == 1), b + 2 < B))
        def _():
            loop(Q, lambda q: load_prev(b + 2, q).start())

    def ahead(t, i):
        b, q = lax.div(t, 2), lax.div(i, G)
        nk = b + 1

        h = lax.rem(t, 2)

        @pl.when(jnp.logical_and(h == jnp.where(b == 0, 1, 0), lax.rem(i, G) == G // 2))
        def _():
            base(nk, q)

        def older(j):
            @pl.when(q == 0)
            def _():
                load_lower(nk, j).wait()

            less_both(nk, j, q)

        @pl.when(jnp.logical_and(h == 1, lax.rem(i, G) >= G - 2))
        def _():
            late = (lax.rem(i, G) == G - 1).astype(jnp.int32)
            loop(jnp.where(late == 1, b, jnp.minimum(b, 1)), older, late if G > 1 else 0)

    def at_tick(n, offset, body):
        p = jnp.maximum(n - offset, 0)
        t, i = lax.div(p, D), lax.rem(p, D)

        @pl.when(jnp.logical_and(n >= offset, jnp.logical_and(t < T, i < S)))
        def _():
            body(t, i)

    def tick(n):
        @pl.when(jnp.logical_and(n >= kappa, lax.rem(jnp.maximum(n - kappa, 0), D) == 0))
        def _():
            t = lax.div(n - kappa, D)

            @pl.when(t < T)
            def _():
                consume(t)

        def first(t, i):
            @pl.when(lax.rem(i, G) == 0)
            def _():
                own(t, lax.div(i, G))

            fetch(t, i)

        at_tick(n, omega, first)

        @pl.when(has_r)
        def _():
            at_tick(n, rho, pass_right)

        def to_left(t, i):
            @pl.when(lax.div(i, G) < need_l)
            def _():
                pass_left(t, i)

        @pl.when(has_l)
        def _():
            at_tick(n, lam, to_left)

        def finish(t, i):
            q = lax.div(i, G)

            @pl.when(jnp.logical_and(lax.rem(i, G) == G - 1, q < need))
            def _():
                solve(t, q)

        at_tick(n, sigma, finish)

        def later(t, i):
            @pl.when(lax.div(t, 2) < B - 1)
            def _():
                ahead(t, i)

        at_tick(n, omega, later)

    loop(ticks, tick)

    def drain(t):
        @pl.when(has_r)
        def _():
            loop(S, lambda i: push_right(t, i).wait_send())

        @pl.when(has_l)
        def _():
            loop(need_l * G, lambda i: push_left(t, i).wait_send())

    loop(T, drain, T - 2)


def local(C, R, H, prev_panel, lower_panel, solved_prev, right_block, block_inverse):
    B, NR, KP = prev_panel.shape
    M = solved_prev.shape[1]
    NC, MH = block_inverse.shape[1], M // 2
    CR, S, G, SB, D = shape_plan(C, R, NR, NC)
    T, Q, NS, X = 2 * B, S // G, NC // SB, max(R - 1, 1)
    pairs = B * (B - 1) // 2
    dma = pltpu.SemaphoreType.DMA
    wide = pltpu.VMEM((T, NR, MH), F32)
    return pl.pallas_call(
        functools.partial(kernel, C, R, H, CR, S, G, SB, D),
        out_shape=pltpu.VMEM((B, NC, M), F32),
        in_specs=[pl.BlockSpec(memory_space=pl.ANY)] * 5,
        out_specs=pl.BlockSpec(memory_space=pltpu.VMEM),
        scratch_shapes=[
            pltpu.VMEM((2, NR, KP), F32),
            pltpu.VMEM((pairs, NR, NC), F32),
            pltpu.VMEM((KP, M), F32),
            pltpu.VMEM((B, Q, NC, CR * G), F32),
            pltpu.VMEM((KP, 2 * M), BF16),
            wide, wide, wide, wide, wide,
            pltpu.VMEM((T, NS, SB, MH), F32),
            pltpu.VMEM((T, X, NS, SB, MH), F32),
            pltpu.VMEM((B, 4, NC, MH), BF16),
            pltpu.VMEM((max(NC, CR * G), MH), F32),
            pltpu.VMEM((NC, MH), F32),
            dma((2, Q)), dma((pairs,)), dma, dma((T,)), dma((B, Q)),
            dma((T, S)), dma((T, S)), dma((T, S)), dma((T, S)),
            dma((T, NS, X)), dma((T, NS, X)), pltpu.SemaphoreType.REGULAR,
        ],
        compiler_params=pltpu.CompilerParams(
            collective_id=0, has_side_effects=True, vmem_limit_bytes=VLIM * 2**20),
    )(prev_panel, jnp.transpose(lower_panel, (0, 2, 1, 3)), solved_prev, right_block, block_inverse)


def solution(mesh):
    return jax.shard_map(
        functools.partial(local, mesh.shape["col"], mesh.shape["row"], mesh.shape["rhs"] if STAGGER else 1),
        mesh=mesh,
        in_specs=(
            P(None, "row", "col"),
            P(None, "row", None, "col"),
            P("col", ("groups", "rhs")),
            P("groups", "row", "rhs"),
            P(None, "col", "row"),
        ),
        out_specs=P("groups", "col", "rhs"),
        check_vma=False,
    )
```

```python
import functools

import jax
import jax.numpy as jnp
from jax import lax
from jax.experimental import pallas as pl
from jax.experimental.pallas import tpu as pltpu
from jax.sharding import PartitionSpec as P

F32, BF16 = jnp.float32, jnp.bfloat16
MESH = pl.DeviceIdType.MESH
HOP = 5
LAM = 4
XLAT = 8
VLIM = 59


def split(value):
    high = value.astype(BF16)
    return high, (value - high.astype(F32)).astype(BF16)


def product(left, both):
    high, low = split(left)
    n = both.shape[1] // 2
    wide = jnp.dot(high, both, preferred_element_type=F32)
    return wide[:, :n] + wide[:, n:] + jnp.dot(low, both[:, :n], preferred_element_type=F32)


def offsets(C, S, c):
    rho, lam = HOP * c, LAM + HOP * (C - 1 - c)
    first, last = c == 0, c == C - 1
    if isinstance(c, int):
        return rho, lam, rho if first else lam if last else min(rho, lam), rho if last else max(rho, lam)
    omega = jnp.where(first, rho, jnp.where(last, lam, jnp.minimum(rho, lam)))
    return rho, lam, omega, jnp.where(last, rho, jnp.maximum(rho, lam))


def shape_plan(C, R, NR, NC):
    CR = min(64, NR)
    S = NR // CR
    G = min(4, S)
    QR, Q = CR * G, S // G
    SB = min(256, NC)

    def fits(D):
        for c in range(C):
            rho, lam, omega, sigma = offsets(C, S, c)
            kappa = G * min(Q, -(-(c + 1) * NC // QR)) - 1 + sigma + XLAT
            until = omega
            if c in (0, C - 1):
                kappa = max(kappa, omega + D + S)
                until = HOP if c == 0 else LAM + HOP
                kappa += 1
            if kappa > 2 * D + until:
                return False
        return True

    D = S
    while not fits(D):
        D += 1
    return CR, S, G, SB, D


def kernel(
    C, R, CR, S, G, SB, D,
    prev_hbm, lower_hbm, sprev_hbm, right_hbm, inv_hbm, out_ref,
    prev, lower, sprev, inv, sprev_both, part, from_l, from_r, to_l, to_r,
    xsend, xrecv, solved, tot, acc,
    prev_sem, lower_sem, sprev_sem, right_sem, inv_sem,
    send_r, recv_l, send_l, recv_r, xs_sem, xr_sem,
):
    T, NR, MH = part.shape
    B = T // 2
    NC = out_ref.shape[1]
    Q, QR, NS = S // G, CR * G, NC // SB
    c, r = lax.axis_index("col"), lax.axis_index("row")
    has_l, has_r = c > 0, c < C - 1
    left, right_of = jnp.maximum(c - 1, 0), jnp.minimum(c + 1, C - 1)

    def need_of(col, row):
        rows = jnp.maximum((col + 1) * NC - row * NR, 0)
        return jnp.minimum(lax.div(rows + QR - 1, QR), Q)

    need, need_l = need_of(c, r), jnp.where(has_l, need_of(c - 1, r), 0)
    rho, lam, omega, sigma = offsets(C, S, c)
    edge = jnp.logical_or(c == 0, jnp.logical_not(has_r))
    inner = jnp.logical_not(edge)
    kappa = G * need_of(c, 0) - 1 + sigma + XLAT
    kappa = jnp.where(edge, jnp.maximum(kappa, omega + D + S), kappa)
    ticks = (T - 1) * D + 1 + jnp.maximum(kappa, S - 1 + jnp.maximum(rho, lam))

    def rows(q):
        return pl.ds(pl.multiple_of(q * QR, QR), QR)

    def piece_rows(i):
        return pl.ds(pl.multiple_of(i * CR, CR), CR)

    def tri(k, j):
        return lax.div(k * (k - 1), 2) + j

    def load_prev(k, q):
        slot = lax.rem(k, 2)
        return pltpu.make_async_copy(prev_hbm.at[k, rows(q)], prev.at[slot, rows(q)], prev_sem.at[slot, q])

    def load_right(t):
        cols = pl.ds(pl.multiple_of(lax.rem(t, 2) * MH, MH), MH)
        return pltpu.make_async_copy(right_hbm.at[lax.div(t, 2), :, cols], from_l.at[t], right_sem.at[t])

    def load_inv(k, q):
        return pltpu.make_async_copy(inv_hbm.at[k, :, rows(q)], inv.at[k, q], inv_sem.at[k, q])

    def load_lower(k, j):
        return pltpu.make_async_copy(lower_hbm.at[k - 1, j], lower.at[tri(k, j)], lower_sem.at[tri(k, j)])

    def loop(n, body, start=0):
        lax.fori_loop(start, n, lambda i, _: (body(i), 0)[1], 0)

    load_sprev = pltpu.make_async_copy(sprev_hbm, sprev, sprev_sem)
    load_sprev.start()
    load_prev(0, 0).start()

    @pl.when(c == 0)
    def _():
        load_right(0).start()

    barrier = pltpu.get_barrier_semaphore()

    @pl.when(has_l)
    def _():
        pl.semaphore_signal(barrier, inc=1, device_id={"col": left}, device_id_type=MESH)

    @pl.when(has_r)
    def _():
        pl.semaphore_signal(barrier, inc=1, device_id={"col": right_of}, device_id_type=MESH)

    for d in range(1, R):
        pl.semaphore_signal(barrier, inc=1, device_id={"row": lax.rem(r + d, R)}, device_id_type=MESH)

    def push_right(t, i):
        return pltpu.make_async_remote_copy(
            src_ref=to_r.at[t, piece_rows(i)], dst_ref=from_l.at[t, piece_rows(i)],
            send_sem=send_r.at[t, i], recv_sem=recv_l.at[t, i],
            device_id={"col": right_of}, device_id_type=MESH)

    def push_left(t, i):
        return pltpu.make_async_remote_copy(
            src_ref=to_l.at[t, piece_rows(i)], dst_ref=from_r.at[t, piece_rows(i)],
            send_sem=send_l.at[t, i], recv_sem=recv_r.at[t, i],
            device_id={"col": left}, device_id_type=MESH)

    def push_x(t, s, d):
        return pltpu.make_async_remote_copy(
            src_ref=xsend.at[t, s], dst_ref=xrecv.at[t, d - 1, s],
            send_sem=xs_sem.at[t, s, d - 1], recv_sem=xr_sem.at[t, s, d - 1],
            device_id={"row": lax.rem(r + d, R)}, device_id_type=MESH)

    def base(k, q):
        load_prev(k, q).wait()
        high, low = split(prev[lax.rem(k, 2), rows(q), :])
        m = sprev_both.shape[1] // 2
        s_hi, s_lo = sprev_both[:, :m], sprev_both[:, m:]
        a = jnp.dot(high, s_hi, preferred_element_type=F32)
        a = a + jnp.dot(high, s_lo, preferred_element_type=F32)
        a = a + jnp.dot(low, s_hi, preferred_element_type=F32)
        part[2 * k, rows(q)] = -a[:, :MH]
        part[2 * k + 1, rows(q)] = -a[:, MH:]

    def less(k, j, h, q):
        both = jnp.concatenate([solved[j, h], solved[j, 2 + h]], axis=1)
        part[2 * k + h, rows(q)] -= product(lower[tri(k, j), rows(q), :], both)

    def less_both(k, j, q):
        s_hi = jnp.concatenate([solved[j, 0], solved[j, 1]], axis=1)
        s_lo = jnp.concatenate([solved[j, 2], solved[j, 3]], axis=1)
        high, low = split(lower[tri(k, j), rows(q), :])
        a = jnp.dot(high, s_hi, preferred_element_type=F32)
        a = a + jnp.dot(high, s_lo, preferred_element_type=F32)
        a = a + jnp.dot(low, s_hi, preferred_element_type=F32)
        part[2 * k, rows(q)] -= a[:, :MH]
        part[2 * k + 1, rows(q)] -= a[:, MH:]

    load_sprev.wait()
    loop(Q, lambda q: load_prev(0, q).start(), 1)

    @pl.when(c == 0)
    def _():
        load_right(1).start()

    m = sprev.shape[1]
    s_hi, s_lo = split(sprev[...])
    sprev_both[:, :m] = s_hi
    sprev_both[:, m:] = s_lo
    base(0, 0)
    pl.semaphore_wait(barrier, has_l.astype(jnp.int32) + has_r.astype(jnp.int32) + (R - 1))

    def consume(t):
        k, h = lax.div(t, 2), lax.rem(t, 2)

        @pl.when(need > 0)
        def _():
            for s in range(NS):
                tot[s * SB:(s + 1) * SB] = xsend[t, s]

        @pl.when(need == 0)
        def _():
            tot[:NC] = jnp.zeros((NC, MH), F32)

        for d in range(1, R):
            @pl.when(need_of(c, lax.rem(r + R - d, R)) > 0)
            def _():
                for s in range(NS):
                    push_x(t, s, d).wait_recv()
                    tot[s * SB:(s + 1) * SB] += xrecv[t, d - 1, s]

            @pl.when(need > 0)
            def _():
                for s in range(NS):
                    push_x(t, s, d).wait_send()

        value = tot[:NC]
        for side in range(2):
            @pl.when(h == side)
            def _():
                out_ref[k, :, side * MH:(side + 1) * MH] = value

        @pl.when(k < B - 1)
        def _():
            solved[k, h], solved[k, 2 + h] = split(value)

    def own(t, q):
        k, h = lax.div(t, 2), lax.rem(t, 2)

        @pl.when(jnp.logical_and(t == 0, q > 0))
        def _():
            base(0, q)

        @pl.when(k > 0)
        def _():
            @pl.when(jnp.logical_and(h == 0, q == 0))
            def _():
                load_lower(k, k - 1).wait()

            less(k, k - 1, h, q)

    def pass_right(t, i):
        @pl.when(has_l)
        def _():
            push_right(t, i).wait_recv()

        @pl.when(jnp.logical_and(c == 0, i == 0))
        def _():
            load_right(t).wait()

        at = piece_rows(i)
        to_r[t, at] = from_l[t, at] + part[t, at]
        push_right(t, i).start()

        @pl.when(t >= 2)
        def _():
            push_right(t - 2, i).wait_send()

    def pass_left(t, i):
        at = piece_rows(i)

        @pl.when(has_r)
        def _():
            push_left(t, i).wait_recv()
            to_l[t, at] = from_r[t, at] + part[t, at]

        @pl.when(jnp.logical_not(has_r))
        def _():
            to_l[t, at] = part[t, at]

        push_left(t, i).start()

        @pl.when(t >= 2)
        def _():
            push_left(t - 2, i).wait_send()

    def solve(t, q):
        k, h = lax.div(t, 2), lax.rem(t, 2)

        @pl.when(jnp.logical_not(has_r))
        def _():
            for g in range(G):
                push_right(t, q * G + g).wait_recv()

        @pl.when(jnp.logical_and(has_r, q >= need_l))
        def _():
            for g in range(G):
                push_left(t, q * G + g).wait_recv()

        @pl.when(h == 0)
        def _():
            load_inv(k, q).wait()

        tot[:QR] = from_l[t, rows(q)] + part[t, rows(q)]

        @pl.when(has_r)
        def _():
            tot[:QR] += from_r[t, rows(q)]

        high, low = split(tot[:QR])
        piece = product(inv[k, q], jnp.concatenate([high, low], axis=1))

        @pl.when(q == 0)
        def _():
            acc[...] = piece

        @pl.when(q > 0)
        def _():
            acc[...] += piece

        for s in range(NS):
            last = jnp.maximum(c * NC + (s + 1) * SB - r * NR, 1) - 1

            @pl.when(q == jnp.minimum(lax.div(last, QR), Q - 1))
            def _():
                xsend[t, s] = acc[s * SB:(s + 1) * SB]
                for d in range(1, R):
                    push_x(t, s, d).start()

    def fetch(t, i):
        b, h = lax.div(t, 2), lax.rem(t, 2)

        @pl.when(jnp.logical_and(h == 0, i == 1))
        def _():
            @pl.when(b == 0)
            def _():
                loop(need, lambda q: load_inv(0, q).start())
                load_lower(1, 0).start()
                loop(Q, lambda q: load_prev(1, q).start())

            @pl.when(b + 1 < B)
            def _():
                loop(need, lambda q: load_inv(b + 1, q).start())

                @pl.when(c == 0)
                def _():
                    load_right(t + 2).start()
                    load_right(t + 3).start()

            @pl.when(b + 2 < B)
            def _():
                loop(b + 2, lambda j: load_lower(b + 2, j).start())

        @pl.when(jnp.logical_and(jnp.logical_and(h == 1, i == 1), b + 2 < B))
        def _():
            loop(Q, lambda q: load_prev(b + 2, q).start())

    def ahead(t, i):
        b, q = lax.div(t, 2), lax.div(i, G)
        nk = b + 1

        h = lax.rem(t, 2)

        @pl.when(jnp.logical_and(h == jnp.where(b == 0, 1, 0), lax.rem(i, G) == G // 2))
        def _():
            base(nk, q)

        def older(j):
            @pl.when(q == 0)
            def _():
                load_lower(nk, j).wait()

            less_both(nk, j, q)

        @pl.when(jnp.logical_and(h == 1, lax.rem(i, G) >= G - 2))
        def _():
            late = (lax.rem(i, G) == G - 1).astype(jnp.int32)
            loop(jnp.where(late == 1, b, jnp.minimum(b, 1)), older, late if G > 1 else 0)

    def at_tick(n, offset, body):
        p = jnp.maximum(n - offset, 0)
        t, i = lax.div(p, D), lax.rem(p, D)

        @pl.when(jnp.logical_and(n >= offset, jnp.logical_and(t < T, i < S)))
        def _():
            body(t, i)

    def emit(t):
        def group(q):
            own(t, q)

            @pl.when(c == 0)
            def _():
                loop(q * G + G, lambda i: pass_right(t, i), q * G)

            @pl.when(jnp.logical_and(jnp.logical_not(has_r), q < need_l))
            def _():
                loop(q * G + G, lambda i: pass_left(t, i), q * G)

        loop(Q, group)

    def tick(n):
        p = n - kappa + 2 * D
        t = lax.div(jnp.maximum(p, 0), D)

        @pl.when(jnp.logical_and(jnp.logical_and(t >= 2, lax.rem(jnp.maximum(p, 0), D) == 0), t < T + 2))
        def _():
            consume(t - 2)

            @pl.when(jnp.logical_and(edge, t < T))
            def _():
                emit(t)

        def first(t, i):
            @pl.when(jnp.logical_and(lax.rem(i, G) == 0, inner))
            def _():
                own(t, lax.div(i, G))

            fetch(t, i)

        at_tick(n, omega, first)

        @pl.when(jnp.logical_and(edge, jnp.logical_and(n >= omega, n < omega + 2)))
        def _():
            emit(n - omega)

        @pl.when(inner)
        def _():
            at_tick(n, rho, pass_right)

        def to_left(t, i):
            @pl.when(lax.div(i, G) < need_l)
            def _():
                pass_left(t, i)

        @pl.when(inner)
        def _():
            at_tick(n, lam, to_left)

        def finish(t, i):
            q = lax.div(i, G)

            @pl.when(jnp.logical_and(lax.rem(i, G) == G - 1, q < need))
            def _():
                solve(t, q)

        at_tick(n, sigma, finish)

        def later(t, i):
            @pl.when(lax.div(t, 2) < B - 1)
            def _():
                ahead(t, i)

        at_tick(n, omega, later)

    loop(ticks, tick)

    def drain(t):
        @pl.when(has_r)
        def _():
            loop(S, lambda i: push_right(t, i).wait_send())

        @pl.when(has_l)
        def _():
            loop(need_l * G, lambda i: push_left(t, i).wait_send())

    loop(T, drain, T - 2)


def local(C, R, prev_panel, lower_panel, solved_prev, right_block, block_inverse):
    B, NR, KP = prev_panel.shape
    M = solved_prev.shape[1]
    NC, MH = block_inverse.shape[1], M // 2
    CR, S, G, SB, D = shape_plan(C, R, NR, NC)
    T, Q, NS, X = 2 * B, S // G, NC // SB, max(R - 1, 1)
    pairs = B * (B - 1) // 2
    dma = pltpu.SemaphoreType.DMA
    wide = pltpu.VMEM((T, NR, MH), F32)
    return pl.pallas_call(
        functools.partial(kernel, C, R, CR, S, G, SB, D),
        out_shape=pltpu.VMEM((B, NC, M), F32),
        in_specs=[pl.BlockSpec(memory_space=pl.ANY)] * 5,
        out_specs=pl.BlockSpec(memory_space=pltpu.VMEM),
        scratch_shapes=[
            pltpu.VMEM((2, NR, KP), F32),
            pltpu.VMEM((pairs, NR, NC), F32),
            pltpu.VMEM((KP, M), F32),
            pltpu.VMEM((B, Q, NC, CR * G), F32),
            pltpu.VMEM((KP, 2 * M), BF16),
            wide, wide, wide, wide, wide,
            pltpu.VMEM((T, NS, SB, MH), F32),
            pltpu.VMEM((T, X, NS, SB, MH), F32),
            pltpu.VMEM((B, 4, NC, MH), BF16),
            pltpu.VMEM((max(NC, CR * G), MH), F32),
            pltpu.VMEM((NC, MH), F32),
            dma((2, Q)), dma((pairs,)), dma, dma((T,)), dma((B, Q)),
            dma((T, S)), dma((T, S)), dma((T, S)), dma((T, S)),
            dma((T, NS, X)), dma((T, NS, X)),
        ],
        compiler_params=pltpu.CompilerParams(
            collective_id=0, has_side_effects=True, vmem_limit_bytes=VLIM * 2**20),
    )(prev_panel, jnp.transpose(lower_panel, (0, 2, 1, 3)), solved_prev, right_block, block_inverse)


def solution(mesh):
    return jax.shard_map(
        functools.partial(local, mesh.shape["col"], mesh.shape["row"]),
        mesh=mesh,
        in_specs=(
            P(None, "row", "col"),
            P(None, "row", None, "col"),
            P("col", ("groups", "rhs")),
            P("groups", "row", "rhs"),
            P(None, "col", "row"),
        ),
        out_specs=P("groups", "col", "rhs"),
        check_vma=False,
    )
```

```python
import functools

import jax
import jax.numpy as jnp
from jax import lax
from jax.experimental import pallas as pl
from jax.experimental.pallas import tpu as pltpu
from jax.sharding import PartitionSpec as P

F32, BF16 = jnp.float32, jnp.bfloat16
MESH = pl.DeviceIdType.MESH
HOP = 5
LAM = 4
XLAT = 8
VLIM = 59


def split(value):
    high = value.astype(BF16)
    return high, (value - high.astype(F32)).astype(BF16)


def product(left, both):
    high, low = split(left)
    n = both.shape[1] // 2
    wide = jnp.dot(high, both, preferred_element_type=F32)
    return wide[:, :n] + wide[:, n:] + jnp.dot(low, both[:, :n], preferred_element_type=F32)


def offsets(C, S, c):
    rho, lam = HOP * c, LAM + HOP * (C - 1 - c)
    first, last = c == 0, c == C - 1
    if isinstance(c, int):
        return rho, lam, rho if first else lam if last else min(rho, lam), rho if last else max(rho, lam)
    omega = jnp.where(first, rho, jnp.where(last, lam, jnp.minimum(rho, lam)))
    return rho, lam, omega, jnp.where(last, rho, jnp.maximum(rho, lam))


def shape_plan(C, R, NR, NC):
    CR = min(64, NR)
    S = NR // CR
    G = min(4, S)
    QR, Q = CR * G, S // G
    SB = min(256, NC)

    def fits(D):
        for c in range(C):
            rho, lam, omega, sigma = offsets(C, S, c)
            kappa = G * min(Q, -(-(c + 1) * NC // QR)) - 1 + sigma + XLAT
            until = omega
            if c in (0, C - 1):
                kappa = max(kappa, omega + D + S)
                until = HOP if c == 0 else LAM + HOP
                kappa += 1
            if kappa > 2 * D + until:
                return False
        return True

    D = S
    while not fits(D):
        D += 1
    return CR, S, G, SB, D


def kernel(
    C, R, CR, S, G, SB, D,
    prev_hbm, lower_hbm, sprev_hbm, right_hbm, inv_hbm, out_ref,
    prev, lower, sprev, inv, sprev_both, part, from_l, from_r, to_l, to_r,
    xsend, xrecv, solved, tot, acc,
    prev_sem, lower_sem, sprev_sem, right_sem, inv_sem,
    send_r, recv_l, send_l, recv_r, xs_sem, xr_sem,
):
    T, NR, MH = part.shape
    B = T // 2
    NC = out_ref.shape[1]
    Q, QR, NS = S // G, CR * G, NC // SB
    c, r = lax.axis_index("col"), lax.axis_index("row")
    has_l, has_r = c > 0, c < C - 1
    left, right_of = jnp.maximum(c - 1, 0), jnp.minimum(c + 1, C - 1)

    def need_of(col, row):
        rows = jnp.maximum((col + 1) * NC - row * NR, 0)
        return jnp.minimum(lax.div(rows + QR - 1, QR), Q)

    need, need_l = need_of(c, r), jnp.where(has_l, need_of(c - 1, r), 0)
    rho, lam, omega, sigma = offsets(C, S, c)
    edge = jnp.logical_or(c == 0, jnp.logical_not(has_r))
    inner = jnp.logical_not(edge)
    kappa = G * need_of(c, 0) - 1 + sigma + XLAT
    kappa = jnp.where(edge, jnp.maximum(kappa, omega + D + S), kappa)
    ticks = (T - 1) * D + 1 + jnp.maximum(kappa, S - 1 + jnp.maximum(rho, lam))

    def rows(q):
        return pl.ds(pl.multiple_of(q * QR, QR), QR)

    def piece_rows(i):
        return pl.ds(pl.multiple_of(i * CR, CR), CR)

    def tri(k, j):
        return lax.div(k * (k - 1), 2) + j

    def load_prev(k, q):
        slot = lax.rem(k, 2)
        return pltpu.make_async_copy(prev_hbm.at[k, rows(q)], prev.at[slot, rows(q)], prev_sem.at[slot, q])

    def load_right(t):
        cols = pl.ds(pl.multiple_of(lax.rem(t, 2) * MH, MH), MH)
        return pltpu.make_async_copy(right_hbm.at[lax.div(t, 2), :, cols], from_l.at[t], right_sem.at[t])

    def load_inv(k, q):
        return pltpu.make_async_copy(inv_hbm.at[k, :, rows(q)], inv.at[k, q], inv_sem.at[k, q])

    def load_lower(k, j):
        return pltpu.make_async_copy(lower_hbm.at[k - 1, j], lower.at[tri(k, j)], lower_sem.at[tri(k, j)])

    def loop(n, body, start=0):
        lax.fori_loop(start, n, lambda i, _: (body(i), 0)[1], 0)

    load_sprev = pltpu.make_async_copy(sprev_hbm, sprev, sprev_sem)
    load_sprev.start()
    load_prev(0, 0).start()

    @pl.when(c == 0)
    def _():
        load_right(0).start()

    barrier = pltpu.get_barrier_semaphore()

    @pl.when(has_l)
    def _():
        pl.semaphore_signal(barrier, inc=1, device_id={"col": left}, device_id_type=MESH)

    @pl.when(has_r)
    def _():
        pl.semaphore_signal(barrier, inc=1, device_id={"col": right_of}, device_id_type=MESH)

    for d in range(1, R):
        pl.semaphore_signal(barrier, inc=1, device_id={"row": lax.rem(r + d, R)}, device_id_type=MESH)

    def push_right(t, i):
        return pltpu.make_async_remote_copy(
            src_ref=to_r.at[t, piece_rows(i)], dst_ref=from_l.at[t, piece_rows(i)],
            send_sem=send_r.at[t, i], recv_sem=recv_l.at[t, i],
            device_id={"col": right_of}, device_id_type=MESH)

    def push_left(t, i):
        return pltpu.make_async_remote_copy(
            src_ref=to_l.at[t, piece_rows(i)], dst_ref=from_r.at[t, piece_rows(i)],
            send_sem=send_l.at[t, i], recv_sem=recv_r.at[t, i],
            device_id={"col": left}, device_id_type=MESH)

    def push_x(t, s, d):
        return pltpu.make_async_remote_copy(
            src_ref=xsend.at[t, s], dst_ref=xrecv.at[t, d - 1, s],
            send_sem=xs_sem.at[t, s, d - 1], recv_sem=xr_sem.at[t, s, d - 1],
            device_id={"row": lax.rem(r + d, R)}, device_id_type=MESH)

    def base(k, q):
        load_prev(k, q).wait()
        high, low = split(prev[lax.rem(k, 2), rows(q), :])
        m = sprev_both.shape[1] // 2
        s_hi, s_lo = sprev_both[:, :m], sprev_both[:, m:]
        a = jnp.dot(high, s_hi, preferred_element_type=F32)
        a = a + jnp.dot(high, s_lo, preferred_element_type=F32)
        a = a + jnp.dot(low, s_hi, preferred_element_type=F32)
        part[2 * k, rows(q)] = -a[:, :MH]
        part[2 * k + 1, rows(q)] = -a[:, MH:]

    def less(k, j, h, q):
        both = jnp.concatenate([solved[j, h], solved[j, 2 + h]], axis=1)
        part[2 * k + h, rows(q)] -= product(lower[tri(k, j), rows(q), :], both)

    def less_both(k, j, q):
        s_hi = jnp.concatenate([solved[j, 0], solved[j, 1]], axis=1)
        s_lo = jnp.concatenate([solved[j, 2], solved[j, 3]], axis=1)
        high, low = split(lower[tri(k, j), rows(q), :])
        a = jnp.dot(high, s_hi, preferred_element_type=F32)
        a = a + jnp.dot(high, s_lo, preferred_element_type=F32)
        a = a + jnp.dot(low, s_hi, preferred_element_type=F32)
        part[2 * k, rows(q)] -= a[:, :MH]
        part[2 * k + 1, rows(q)] -= a[:, MH:]

    load_sprev.wait()
    loop(Q, lambda q: load_prev(0, q).start(), 1)

    @pl.when(c == 0)
    def _():
        load_right(1).start()

    m = sprev.shape[1]
    s_hi, s_lo = split(sprev[...])
    sprev_both[:, :m] = s_hi
    sprev_both[:, m:] = s_lo
    base(0, 0)
    pl.semaphore_wait(barrier, has_l.astype(jnp.int32) + has_r.astype(jnp.int32) + (R - 1))

    def consume(t):
        k, h = lax.div(t, 2), lax.rem(t, 2)

        @pl.when(need > 0)
        def _():
            for s in range(NS):
                tot[s * SB:(s + 1) * SB] = xsend[t, s]

        @pl.when(need == 0)
        def _():
            tot[:NC] = jnp.zeros((NC, MH), F32)

        for d in range(1, R):
            @pl.when(need_of(c, lax.rem(r + R - d, R)) > 0)
            def _():
                for s in range(NS):
                    push_x(t, s, d).wait_recv()
                    tot[s * SB:(s + 1) * SB] += xrecv[t, d - 1, s]

            @pl.when(need > 0)
            def _():
                for s in range(NS):
                    push_x(t, s, d).wait_send()

        value = tot[:NC]
        for side in range(2):
            @pl.when(h == side)
            def _():
                out_ref[k, :, side * MH:(side + 1) * MH] = value

        @pl.when(k < B - 1)
        def _():
            solved[k, h], solved[k, 2 + h] = split(value)

    def own(t, q):
        k, h = lax.div(t, 2), lax.rem(t, 2)

        @pl.when(jnp.logical_and(t == 0, q > 0))
        def _():
            base(0, q)

        @pl.when(k > 0)
        def _():
            @pl.when(jnp.logical_and(h == 0, q == 0))
            def _():
                load_lower(k, k - 1).wait()

            less(k, k - 1, h, q)

    def pass_right(t, i):
        @pl.when(has_l)
        def _():
            push_right(t, i).wait_recv()

        @pl.when(jnp.logical_and(c == 0, i == 0))
        def _():
            load_right(t).wait()

        at = piece_rows(i)
        to_r[t, at] = from_l[t, at] + part[t, at]
        push_right(t, i).start()

        @pl.when(t >= 2)
        def _():
            push_right(t - 2, i).wait_send()

    def pass_left(t, i):
        at = piece_rows(i)

        @pl.when(has_r)
        def _():
            push_left(t, i).wait_recv()
            to_l[t, at] = from_r[t, at] + part[t, at]

        @pl.when(jnp.logical_not(has_r))
        def _():
            to_l[t, at] = part[t, at]

        push_left(t, i).start()

        @pl.when(t >= 2)
        def _():
            push_left(t - 2, i).wait_send()

    def solve(t, q):
        k, h = lax.div(t, 2), lax.rem(t, 2)

        @pl.when(jnp.logical_not(has_r))
        def _():
            for g in range(G):
                push_right(t, q * G + g).wait_recv()

        @pl.when(jnp.logical_and(has_r, q >= need_l))
        def _():
            for g in range(G):
                push_left(t, q * G + g).wait_recv()

        @pl.when(h == 0)
        def _():
            load_inv(k, q).wait()

        tot[:QR] = from_l[t, rows(q)] + part[t, rows(q)]

        @pl.when(has_r)
        def _():
            tot[:QR] += from_r[t, rows(q)]

        high, low = split(tot[:QR])
        both = jnp.concatenate([high, low], axis=1)
        for s in range(NS):
            at = slice(s * SB, (s + 1) * SB)
            piece = product(inv[k, q, at], both)

            @pl.when(q == 0)
            def _():
                acc[at] = piece

            @pl.when(q > 0)
            def _():
                acc[at] += piece

            last = jnp.maximum(c * NC + (s + 1) * SB - r * NR, 1) - 1

            @pl.when(q == jnp.minimum(lax.div(last, QR), Q - 1))
            def _():
                xsend[t, s] = acc[at]
                for d in range(1, R):
                    push_x(t, s, d).start()

    def fetch(t, i):
        b, h = lax.div(t, 2), lax.rem(t, 2)

        @pl.when(jnp.logical_and(h == 0, i == 1))
        def _():
            @pl.when(b == 0)
            def _():
                loop(need, lambda q: load_inv(0, q).start())
                load_lower(1, 0).start()
                loop(Q, lambda q: load_prev(1, q).start())

            @pl.when(b + 1 < B)
            def _():
                loop(need, lambda q: load_inv(b + 1, q).start())

                @pl.when(c == 0)
                def _():
                    load_right(t + 2).start()
                    load_right(t + 3).start()

            @pl.when(b + 2 < B)
            def _():
                loop(b + 2, lambda j: load_lower(b + 2, j).start())

        @pl.when(jnp.logical_and(jnp.logical_and(h == 1, i == 1), b + 2 < B))
        def _():
            loop(Q, lambda q: load_prev(b + 2, q).start())

    def ahead(t, i):
        b, q = lax.div(t, 2), lax.div(i, G)
        nk = b + 1

        h = lax.rem(t, 2)

        @pl.when(jnp.logical_and(h == jnp.where(b == 0, 1, 0), lax.rem(i, G) == G // 2))
        def _():
            base(nk, q)

        def older(j):
            @pl.when(q == 0)
            def _():
                load_lower(nk, j).wait()

            less_both(nk, j, q)

        @pl.when(jnp.logical_and(h == 1, lax.rem(i, G) >= G - 2))
        def _():
            late = (lax.rem(i, G) == G - 1).astype(jnp.int32)
            loop(jnp.where(late == 1, b, jnp.minimum(b, 1)), older, late if G > 1 else 0)

    def at_tick(n, offset, body):
        p = jnp.maximum(n - offset, 0)
        t, i = lax.div(p, D), lax.rem(p, D)

        @pl.when(jnp.logical_and(n >= offset, jnp.logical_and(t < T, i < S)))
        def _():
            body(t, i)

    def emit(t):
        def group(q):
            own(t, q)

            @pl.when(c == 0)
            def _():
                loop(q * G + G, lambda i: pass_right(t, i), q * G)

            @pl.when(jnp.logical_and(jnp.logical_not(has_r), q < need_l))
            def _():
                loop(q * G + G, lambda i: pass_left(t, i), q * G)

        loop(Q, group)

    def tick(n):
        p = n - kappa + 2 * D
        t = lax.div(jnp.maximum(p, 0), D)

        @pl.when(jnp.logical_and(jnp.logical_and(t >= 2, lax.rem(jnp.maximum(p, 0), D) == 0), t < T + 2))
        def _():
            consume(t - 2)

            @pl.when(jnp.logical_and(edge, t < T))
            def _():
                emit(t)

        def first(t, i):
            @pl.when(jnp.logical_and(lax.rem(i, G) == 0, inner))
            def _():
                own(t, lax.div(i, G))

            fetch(t, i)

        at_tick(n, omega, first)

        @pl.when(jnp.logical_and(edge, jnp.logical_and(n >= omega, n < omega + 2)))
        def _():
            emit(n - omega)

        @pl.when(inner)
        def _():
            at_tick(n, rho, pass_right)

        def to_left(t, i):
            @pl.when(lax.div(i, G) < need_l)
            def _():
                pass_left(t, i)

        @pl.when(inner)
        def _():
            at_tick(n, lam, to_left)

        def finish(t, i):
            q = lax.div(i, G)

            @pl.when(jnp.logical_and(lax.rem(i, G) == G - 1, q < need))
            def _():
                solve(t, q)

        at_tick(n, sigma, finish)

        def later(t, i):
            @pl.when(lax.div(t, 2) < B - 1)
            def _():
                ahead(t, i)

        at_tick(n, omega, later)

    loop(ticks, tick)

    def drain(t):
        @pl.when(has_r)
        def _():
            loop(S, lambda i: push_right(t, i).wait_send())

        @pl.when(has_l)
        def _():
            loop(need_l * G, lambda i: push_left(t, i).wait_send())

    loop(T, drain, T - 2)


def local(C, R, prev_panel, lower_panel, solved_prev, right_block, block_inverse):
    B, NR, KP = prev_panel.shape
    M = solved_prev.shape[1]
    NC, MH = block_inverse.shape[1], M // 2
    CR, S, G, SB, D = shape_plan(C, R, NR, NC)
    T, Q, NS, X = 2 * B, S // G, NC // SB, max(R - 1, 1)
    pairs = B * (B - 1) // 2
    dma = pltpu.SemaphoreType.DMA
    wide = pltpu.VMEM((T, NR, MH), F32)
    return pl.pallas_call(
        functools.partial(kernel, C, R, CR, S, G, SB, D),
        out_shape=pltpu.VMEM((B, NC, M), F32),
        in_specs=[pl.BlockSpec(memory_space=pl.ANY)] * 5,
        out_specs=pl.BlockSpec(memory_space=pltpu.VMEM),
        scratch_shapes=[
            pltpu.VMEM((2, NR, KP), F32),
            pltpu.VMEM((pairs, NR, NC), F32),
            pltpu.VMEM((KP, M), F32),
            pltpu.VMEM((B, Q, NC, CR * G), F32),
            pltpu.VMEM((KP, 2 * M), BF16),
            wide, wide, wide, wide, wide,
            pltpu.VMEM((T, NS, SB, MH), F32),
            pltpu.VMEM((T, X, NS, SB, MH), F32),
            pltpu.VMEM((B, 4, NC, MH), BF16),
            pltpu.VMEM((max(NC, CR * G), MH), F32),
            pltpu.VMEM((NC, MH), F32),
            dma((2, Q)), dma((pairs,)), dma, dma((T,)), dma((B, Q)),
            dma((T, S)), dma((T, S)), dma((T, S)), dma((T, S)),
            dma((T, NS, X)), dma((T, NS, X)),
        ],
        compiler_params=pltpu.CompilerParams(
            collective_id=0, has_side_effects=True, vmem_limit_bytes=VLIM * 2**20),
    )(prev_panel, jnp.transpose(lower_panel, (0, 2, 1, 3)), solved_prev, right_block, block_inverse)


def solution(mesh):
    return jax.shard_map(
        functools.partial(local, mesh.shape["col"], mesh.shape["row"]),
        mesh=mesh,
        in_specs=(
            P(None, "row", "col"),
            P(None, "row", None, "col"),
            P("col", ("groups", "rhs")),
            P("groups", "row", "rhs"),
            P(None, "col", "row"),
        ),
        out_specs=P("groups", "col", "rhs"),
        check_vma=False,
    )
```
